32 devices in a mesh: dp: 2 (over x), ctx: 16 (over z, y, core).
Axes of the slice: x: 2, y: 2, z: 4, core: 2. Of those that a mesh axis runs over, the one named last changes fastest.
Arguments:
- features: bfloat16 [2, 2048, 1536], P('dp', 'ctx'), may hold values from -500 to 500
- gain: float32 [1536], replicated, may hold values from 0.1 to 1.9
- conv_weight: bfloat16 [5, 1536, 768], replicated, may hold values from -0.0625 to 0.0625
- cotangent: bfloat16 [2, 2048, 768], P('dp', 'ctx'), may hold values from -15 to 15
Outputs:
- convolved: bfloat16 [2, 2048, 768], P('dp', 'ctx')
- input_grad: bfloat16 [2, 2048, 1536], P('dp', 'ctx')
- gain_grad: float32 [1536], replicated
The draws below stay inside these ranges and needn't reach their ends.
All inputs are finite; a program needn't handle non-finite values.
Results may differ from the reference program's by a relative error of at most 0.0054.
Values may be sent and summed in bfloat16 or wider, within the bound.
A program may use at most 64 MiB of HBM per device.

```python
import math
import jax
import jax.numpy as jnp
from jax import lax

CH = 1536
COUT = 768
KERNEL_TAPS = 5
LEN = 2048
DILATION_STEP = 256
BATCH = 2


def draw_features(key, part):
    first_key, second_key, third_key = jax.random.split(jax.random.fold_in(key, 11), 3)
    base = jnp.clip(jax.random.normal(first_key, (BATCH, LEN, CH), jnp.float32), -5.0, 5.0)
    row_scale = jnp.exp(jax.random.uniform(second_key, (BATCH, LEN, 1), jnp.float32, 0.0, math.log(10.0)))
    column_scale = jnp.exp(jax.random.uniform(third_key, (1, 1, CH), jnp.float32, 0.0, math.log(10.0)))
    return (base * row_scale * column_scale).astype(jnp.bfloat16)


def draw_cotangent(key, part):
    first_key = jax.random.fold_in(jax.random.fold_in(key, 23), 0)
    position = jnp.arange(LEN, dtype=jnp.float32) / max(LEN - 1, 1)
    rising = jnp.exp(math.log(3.0) * position)
    base = jnp.clip(jax.random.normal(first_key, (BATCH, LEN, COUT), jnp.float32), -5.0, 5.0)
    return (base * rising[None, :, None]).astype(jnp.bfloat16)


def noise(own_key, shape, width, most, kind=jnp.bfloat16):
    return jnp.clip(width * jax.random.normal(own_key, shape, jnp.float32), -most, most).astype(kind)


def setup_inputs(seed: int = 0) -> dict:
    key_list = jax.random.split(jax.random.key(seed), 5)
    features = draw_features(jax.random.fold_in(key_list[4], 71), 0)
    gain = jnp.clip(1.0 + 0.18 * jax.random.normal(key_list[1], (CH,), jnp.float32), 0.1, 1.9)
    conv_weight = noise(key_list[2], (KERNEL_TAPS, CH, COUT), (KERNEL_TAPS * CH) ** -0.5, 0.0625)
    cotangent = draw_cotangent(jax.random.fold_in(key_list[4], 71), 0)
    return {"features": features, "gain": gain, "conv_weight": conv_weight, "cotangent": cotangent}


EPS = 1e-06

def activate(values):
    return jax.nn.gelu(values, approximate=True)

def shifted(values, strand_heading):
    reach_length = KERNEL_TAPS // 2 * DILATION_STEP
    padded = jnp.pad(values, ((0, 0), (reach_length, reach_length), (0, 0)))
    pieces = []
    for bin_displacement in range(KERNEL_TAPS):
        start_position = reach_length + strand_heading * (bin_displacement - KERNEL_TAPS // 2) * DILATION_STEP
        pieces.append(padded[:, start_position:start_position + LEN, :])
    return pieces

def apply_forward(pieces, weight):
    lead = pieces[0].shape[0]
    middle = pieces[0].shape[1]
    total = jnp.zeros((lead * middle, weight.shape[2]), jnp.float32)
    for tap_index in range(KERNEL_TAPS):
        flat_rows = pieces[tap_index].reshape(lead * middle, pieces[tap_index].shape[2])
        total = total + jnp.dot(flat_rows, weight[tap_index], preferred_element_type=jnp.float32)
    return total.reshape(lead, middle, weight.shape[2])

def apply_backward(pieces, weight):
    lead = pieces[0].shape[0]
    middle = pieces[0].shape[1]
    total = jnp.zeros((lead * middle, weight.shape[1]), jnp.float32)
    for tap_index in range(KERNEL_TAPS):
        flat_rows = pieces[tap_index].reshape(lead * middle, pieces[tap_index].shape[2])
        total = total + lax.dot_general(flat_rows, weight[tap_index], (((1,), (1,)), ((), ())), preferred_element_type=jnp.float32)
    return total.reshape(lead, middle, weight.shape[1])

def reference(features, gain, conv_weight, cotangent):
    wide = features.astype(jnp.float32)
    inv_rms = lax.rsqrt(lax.optimization_barrier(jnp.mean(wide * wide, axis=-1, keepdims=True)) + EPS)
    normed = wide * inv_rms
    scaled = normed * gain
    hidden = activate(scaled).astype(jnp.bfloat16)
    forward_term = apply_forward(shifted(hidden, 1), conv_weight)
    turned = apply_forward(shifted(hidden[:, ::-1, ::-1], 1), conv_weight).astype(jnp.bfloat16)
    reverse_term = turned[:, ::-1, ::-1]
    convolved = (forward_term + reverse_term.astype(jnp.float32)).astype(jnp.bfloat16)
    back_forward = apply_backward(shifted(cotangent, -1), conv_weight)
    back_turned = apply_backward(shifted(cotangent[:, ::-1, ::-1], -1), conv_weight).astype(jnp.bfloat16)
    grad_hidden = back_forward + back_turned[:, ::-1, ::-1].astype(jnp.float32)
    _, pullback = jax.vjp(activate, scaled)
    grad_scaled = pullback(grad_hidden)[0]
    gain_grad = lax.optimization_barrier(jnp.sum(grad_scaled * normed, axis=(0, 1))) / math.sqrt(BATCH * LEN)
    grad_normed = grad_scaled * gain
    spread_term = lax.optimization_barrier(jnp.mean(grad_normed * normed, axis=-1, keepdims=True))
    input_grad = (inv_rms * (grad_normed - normed * spread_term)).astype(jnp.bfloat16)
    return (convolved, input_grad, gain_grad)
```

```python
import functools
import math

import jax
import jax.numpy as jnp
from jax import lax
from jax.experimental import pallas as pl
from jax.experimental.pallas import tpu as pltpu
from jax.sharding import PartitionSpec as P

TAPS = 5
MID = TAPS // 2
SPAN = 8
EPS = 1e-06
TILE = 256
CHUNK = 16
LANES = 128
ROOT = math.sqrt(2.0 / math.pi)
CUBE = 0.044715
MESH = pl.DeviceIdType.MESH
ORDER = (1, 3, 0, 4, 2)
PARTNER, UP, DOWN = range(3)


def body(n_dp, n_ctx, rows_total, feat, gain_in, w, ct, conv_out, grad_out, gain_out,
         gain_ref, gain_v, acc, slope_gain, slope_normed, wv, xv, hh, fa, fb, csend, crecv, via, gg, flip_ref, inv_ref, spread_ref,
         part, sum1, sum2,
         w_sem, x_sem, g_sem, v_sem, ct_ssem, ct_rsem, c_ssem, c_rsem, s1_ssem, s1_rsem, s2_ssem, s2_rsem, know):
    rows, ch = xv.shape
    cout = ct.shape[-1]
    cut = rows * 5 // 8 // 16 * 16
    first, last, whole = pl.ds(0, cut), pl.ds(cut, rows - cut), pl.ds(0, rows)
    hops = n_ctx // SPAN
    me_dp = lax.axis_index("dp")
    me = lax.axis_index("ctx")
    high = SPAN // 2
    group1 = n_dp * hops * 2

    pos = me // hops
    odd = lax.rem(pos, 2)
    side = 2 * odd - 1
    pair = pos // 2
    near = me_dp * hops + lax.rem(me, hops)
    slot1 = odd * (n_dp * hops) + near

    def device(step):
        return {"dp": me_dp, "ctx": me + step * hops}

    def inside(step):
        return jnp.logical_and(pos + step >= 0, pos + step < SPAN)

    partner, up, down = device(-side), device(2 * side), device(-2 * side)
    has_up, has_down = inside(2 * side), inside(-2 * side)
    k_partner, k_diag, k_up, k_down = MID + side, MID - side, MID - 2 * side, MID + 2 * side

    copies_w = {}
    x_copy = pltpu.make_async_copy(feat.at[0], xv, x_sem)
    x_copy.start()
    v_copy = pltpu.make_async_copy(gain_in, gain_v, v_sem)
    v_copy.start()
    for k in ORDER:
        copies_w[k] = pltpu.make_async_copy(w.at[k], wv.at[k], w_sem.at[k])
        copies_w[k].start()
    g_copy = pltpu.make_async_copy(ct.at[0], gg.at[MID, whole], g_sem)
    g_copy.start()

    def peer1(j):
        other = lax.rem(slot1 + j, group1)
        rest = lax.rem(other, n_dp * hops)
        return {"dp": rest // hops, "ctx": (2 * pair + other // (n_dp * hops)) * hops + lax.rem(rest, hops)}

    def same_position(j):
        rest = lax.rem(near + j, n_dp * hops)
        return {"dp": rest // hops, "ctx": pos * hops + lax.rem(rest, hops)}

    def peer2(j):
        other = lax.rem(pair + j, high)
        return {"dp": me_dp, "ctx": (2 * other + odd) * hops + lax.rem(me, hops)}

    barrier = pltpu.get_barrier_semaphore()
    pl.semaphore_signal(barrier, inc=1, device_id=partner, device_id_type=MESH)
    @pl.when(has_up)
    def _():
        pl.semaphore_signal(barrier, inc=1, device_id=up, device_id_type=MESH)
    @pl.when(has_down)
    def _():
        pl.semaphore_signal(barrier, inc=1, device_id=down, device_id_type=MESH)
    for j in range(1, n_dp * hops):
        pl.semaphore_signal(barrier, inc=1, device_id=same_position(j), device_id_type=MESH)
    far = has_up.astype(jnp.int32) + has_down.astype(jnp.int32)
    count = n_dp * hops + far

    def move(src, dst, ssem, rsem, target):
        return pltpu.make_async_remote_copy(
            src_ref=src, dst_ref=dst, send_sem=ssem, recv_sem=rsem, device_id=target, device_id_type=MESH)

    def ct_move(n, src, slot, part_rows, target):
        return move(src.at[part_rows], gg.at[slot, part_rows], ct_ssem.at[n], ct_rsem.at[n], target)

    mine = ct.at[0]
    ct_partner = (ct_move(0, mine, k_diag, first, partner), ct_move(1, mine, k_diag, last, partner))
    ct_up = (ct_move(2, mine, k_down, first, up), ct_move(3, mine, k_down, last, up))
    ct_down = ct_move(4, mine, k_up, whole, down)
    ct_via_down = ct_move(5, gg.at[k_partner], k_diag, first, down)
    ct_via_partner = ct_move(6, gg.at[k_down], k_partner, last, partner)

    def c_move(n, k, dst, part_rows, target):
        return move(csend.at[k, part_rows], dst.at[part_rows], c_ssem.at[n], c_rsem.at[n], target)

    c_diag_up = c_move(0, k_diag, via, first, up)
    c_diag_partner = c_move(1, k_diag, via, last, partner)
    c_partner = (c_move(2, k_partner, crecv.at[PARTNER], first, partner),
                 c_move(3, k_partner, crecv.at[PARTNER], last, partner))
    c_down = (c_move(4, k_down, crecv.at[UP], first, down), c_move(5, k_down, crecv.at[UP], last, down))
    c_up = c_move(6, k_up, crecv.at[DOWN], whole, up)

    @pl.when(jnp.logical_not(has_up))
    def _():
        gg[k_up, whole, :] = jnp.zeros((rows, cout), jnp.bfloat16)
        gg[k_diag, whole, :] = jnp.zeros((rows, cout), jnp.bfloat16)
        crecv[UP] = jnp.zeros((rows, cout), jnp.bfloat16)
    @pl.when(jnp.logical_not(has_down))
    def _():
        gg[k_down, whole, :] = jnp.zeros((rows, cout), jnp.bfloat16)
        crecv[DOWN] = jnp.zeros((rows, cout), jnp.bfloat16)
        via[...] = jnp.zeros((rows, cout), jnp.bfloat16)

    r_iota = lax.broadcasted_iota(jnp.int32, (TILE, TILE), 0)
    c_iota = lax.broadcasted_iota(jnp.int32, (TILE, TILE), 1)
    flip_ref[...] = jnp.where(r_iota + c_iota == TILE - 1, 1.0, 0.0).astype(jnp.bfloat16)

    def flip_all(blocks):
        turned = jnp.dot(jnp.concatenate(blocks[::-1], axis=0), flip_ref[...], preferred_element_type=jnp.float32)
        return [turned[n * rows:(n + 1) * rows] for n in range(len(blocks))]

    n_out, n_in = cout // TILE, ch // TILE
    top, bottom = pl.ds(0, rows), pl.ds(rows, rows)
    tile = [pl.ds(j * TILE, TILE) for j in range(max(n_out, n_in))]

    v_copy.wait()
    gain_ref[...] = gain_v[...].reshape(1, ch)

    x_copy.wait()

    def activate(i):
        here = pl.ds(pl.multiple_of(i * CHUNK, CHUNK), CHUNK)
        wide = xv[here, :].astype(jnp.float32)
        inv = lax.rsqrt(jnp.mean(wide * wide, axis=-1, keepdims=True) + EPS)
        inv_ref[here, :] = inv
        gain = gain_ref[...]
        normed = wide * inv
        v = normed * gain
        square = v * v
        t = jnp.tanh(v * (ROOT + (ROOT * CUBE) * square))
        plus = 0.5 + 0.5 * t
        hh[here, :] = (v * plus).astype(jnp.bfloat16)
        slope = plus + v * (plus * (1.0 - t)) * (ROOT + (3.0 * ROOT * CUBE) * square)
        slope_gain[here, :] = slope * gain
        slope_normed[here, :] = slope * normed

    half = rows // CHUNK // 2
    pl.loop(0, half, unroll=2)(activate)

    pl.semaphore_wait(barrier, count)
    ct_partner[0].start()
    @pl.when(has_up)
    def _():
        ct_up[1].start()
    @pl.when(has_down)
    def _():
        ct_down.start()
    ct_partner[1].start()
    @pl.when(has_up)
    def _():
        ct_up[0].start()

    pl.loop(half, rows // CHUNK, unroll=2)(activate)

    for j, block in enumerate(flip_all([hh[top, tile[j]] for j in range(n_in)])):
        hh[bottom, tile[j]] = block.astype(jnp.bfloat16)

    def forward(k):
        for j in range(n_out):
            res = jnp.dot(hh[...], wv[k, :, tile[j]], preferred_element_type=jnp.float32)
            fa[k, :, tile[j]] = res[:rows]
            fb[k, :, tile[j]] = res[rows:].astype(jnp.bfloat16)

    def join(k):
        for j, block in enumerate(flip_all([fb[TAPS - 1 - k, :, tile[j]] for j in range(n_out)])):
            total = fa[k, :, tile[j]] + block
            fa[k, :, tile[j]] = total
            csend[k, :, tile[j]] = total.astype(jnp.bfloat16)

    def merge(k, part_rows):
        csend[k, part_rows, :] = (fa[k, part_rows, :] + via[part_rows, :].astype(jnp.float32)).astype(jnp.bfloat16)

    def flip_tap(k):
        for j, block in enumerate(flip_all([gg[k, top, tile[j]] for j in range(n_out)])):
            gg[TAPS - 1 - k, bottom, tile[j]] = block.astype(jnp.bfloat16)

    def backward(j, taps):
        return sum(lax.dot_general(
            gg[k], wv[k, tile[j], :], (((1,), (1,)), ((), ())), preferred_element_type=jnp.float32) for k in taps)

    for k in (1, 3):
        copies_w[k].wait()
    for k in (1, 3):
        forward(k)
    for k in (1, 3):
        join(k)
    @pl.when(has_up)
    def _():
        c_diag_up.start()
        c_diag_partner.start()
    c_partner[1].start()

    for k in (0, 4, 2):
        copies_w[k].wait()
    g_copy.wait()
    for k in (0, 4):
        forward(k)
    flip_tap(MID)
    for k in (0, 4):
        join(k)
    @pl.when(has_up)
    def _():
        c_up.start()
    @pl.when(has_down)
    def _():
        c_down[0].start()

    ct_partner[0].wait_recv()
    @pl.when(has_down)
    def _():
        ct_via_down.start()
        ct_up[1].wait_recv()
        ct_via_partner.start()

    for j in range(n_in):
        acc[:, tile[j]] = backward(j, (MID,))

    @pl.when(has_up)
    def _():
        ct_down.wait_recv()
    @pl.when(has_down)
    def _():
        ct_up[0].wait_recv()
    for k in (0, 4):
        flip_tap(k)
    for j in range(n_in):
        acc[:, tile[j]] = acc[:, tile[j]] + backward(j, (0, 4))
    @pl.when(has_up)
    def _():
        pl.semaphore_signal(know, inc=1, device_id=up, device_id_type=MESH)
    @pl.when(has_down)
    def _():
        pl.semaphore_signal(know, inc=1, device_id=down, device_id_type=MESH)

    ct_partner[1].wait_recv()
    @pl.when(has_up)
    def _():
        ct_via_down.wait_recv()
        ct_via_partner.wait_recv()
    for k in (1, 3):
        flip_tap(k)

    spread = jnp.zeros((rows, LANES), jnp.float32)
    for j in range(n_in // 2):
        pair_of = (j, n_in - 1 - j)
        totals = [acc[:, tile[i]] + backward(i, (1, 3)) for i in pair_of]
        turned = flip_all([total[rows:].astype(jnp.bfloat16) for total in totals])
        for i, total, block in zip(pair_of, totals, turned):
            grad = total[:rows] + block
            mixed = grad * slope_normed[:, tile[i]]
            part[:, tile[i]] = jnp.sum(mixed.reshape(rows // 8, 8, TILE), axis=0)
            acc[top, tile[i]] = grad * slope_gain[:, tile[i]]
            mixed = mixed * gain_ref[:, tile[i]]
            spread = spread + sum(mixed[:, n:n + LANES] for n in range(0, TILE, LANES))
    sum1[slot1] = jnp.sum(part[...], axis=0, keepdims=True)

    def s1_copy(j):
        return move(sum1.at[slot1], sum1.at[slot1], s1_ssem.at[j], s1_rsem.at[j], peer1(j))

    def s1_arrival(j):
        sender = lax.rem(slot1 + group1 - j, group1)
        return move(sum1.at[sender], sum1.at[sender], s1_ssem.at[j], s1_rsem.at[j], peer1(j))

    for j in range(1, group1):
        s1_copy(j).start()
    spread_ref[...] = jnp.sum(spread, axis=-1, keepdims=True) * (1.0 / ch)

    @pl.when(has_down)
    def _():
        c_diag_up.wait_recv()
    merge(k_partner, first)
    c_partner[0].start()
    @pl.when(has_down)
    def _():
        c_diag_partner.wait_recv()
        merge(k_down, last)
        c_down[1].start()
    forward(MID)

    @pl.loop(0, rows // CHUNK, unroll=2)
    def _(i):
        here = pl.ds(pl.multiple_of(i * CHUNK, CHUNK), CHUNK)
        inv = inv_ref[here, :]
        normed = xv[here, :].astype(jnp.float32) * inv
        grad_out[0, here, :] = (inv * (acc[here, :] - normed * spread_ref[here, :])).astype(jnp.bfloat16)

    for j in range(1, group1):
        s1_arrival(j).wait_recv()
    sum2[pair] = jnp.sum(sum1[...], axis=0)

    def s2_copy(j):
        return move(sum2.at[pair], sum2.at[pair], s2_ssem.at[j], s2_rsem.at[j], peer2(j))

    def s2_arrival(j):
        sender = lax.rem(pair + high - j, high)
        return move(sum2.at[sender], sum2.at[sender], s2_ssem.at[j], s2_rsem.at[j], peer2(j))

    pl.semaphore_wait(know, far)
    for j in range(1, high):
        s2_copy(j).start()

    c_partner[0].wait_recv()
    c_partner[1].wait_recv()
    @pl.when(has_up)
    def _():
        c_down[0].wait_recv()
        c_down[1].wait_recv()
    @pl.when(has_down)
    def _():
        c_up.wait_recv()

    for j, block in enumerate(flip_all([fb[MID, :, tile[j]] for j in range(n_out)])):
        total = fa[MID, :, tile[j]] + block
        for role in (PARTNER, UP, DOWN):
            total = total + crecv[role, :, tile[j]].astype(jnp.float32)
        conv_out[0, :, tile[j]] = total.astype(jnp.bfloat16)

    for j in range(1, high):
        s2_arrival(j).wait_recv()
    gain_out[...] = jnp.sum(sum2[...], axis=0) * (1.0 / math.sqrt(rows_total))

    for copy in (*ct_partner, *c_partner):
        copy.wait_send()
    @pl.when(has_up)
    def _():
        for copy in (*ct_up, c_diag_up, c_diag_partner, c_up):
            copy.wait_send()
    @pl.when(has_down)
    def _():
        for copy in (ct_down, ct_via_down, ct_via_partner, *c_down):
            copy.wait_send()
    for j in range(1, group1):
        s1_copy(j).wait_send()
    for j in range(1, high):
        s2_copy(j).wait_send()


def hand_over(conv, grad, total, conv_out, grad_out, total_out, sems):
    copies = [pltpu.make_async_copy(src, dst, sems.at[n])
              for n, (src, dst) in enumerate(((grad, grad_out), (conv, conv_out)))]
    for copy in copies:
        copy.start()
    total_out[...] = total[...].reshape(total_out.shape)
    for copy in copies:
        copy.wait()


def per_device(features, gain, conv_weight, cotangent):
    n_dp, n_ctx = lax.axis_size("dp"), lax.axis_size("ctx")
    lead, rows, ch = features.shape
    cout = cotangent.shape[-1]
    high = SPAN // 2
    group1 = n_dp * (n_ctx // SPAN) * 2
    rows_total = lead * rows * n_dp * n_ctx
    hbm_spec = pl.BlockSpec(memory_space=pltpu.HBM)
    vmem_spec = pl.BlockSpec(memory_space=pltpu.VMEM)
    bf16, f32 = jnp.bfloat16, jnp.float32
    dma = pltpu.SemaphoreType.DMA
    conv, grad, total = pl.pallas_call(
        functools.partial(body, n_dp, n_ctx, rows_total),
        out_shape=(
            jax.ShapeDtypeStruct((lead, rows, cout), bf16),
            jax.ShapeDtypeStruct((lead, rows, ch), bf16),
            jax.ShapeDtypeStruct((1, ch), f32),
        ),
        in_specs=[hbm_spec] * 4,
        out_specs=(vmem_spec, vmem_spec, vmem_spec),
        scratch_shapes=[
            pltpu.VMEM((1, ch), f32),
            pltpu.VMEM((ch,), f32),
            pltpu.VMEM((2 * rows, ch), f32),
            pltpu.VMEM((rows, ch), f32),
            pltpu.VMEM((rows, ch), f32),
            pltpu.VMEM((TAPS, ch, cout), bf16),
            pltpu.VMEM((rows, ch), bf16),
            pltpu.VMEM((2 * rows, ch), bf16),
            pltpu.VMEM((TAPS, rows, cout), f32),
            pltpu.VMEM((TAPS, rows, cout), bf16),
            pltpu.VMEM((TAPS, rows, cout), bf16),
            pltpu.VMEM((3, rows, cout), bf16),
            pltpu.VMEM((rows, cout), bf16),
            pltpu.VMEM((TAPS, 2 * rows, cout), bf16),
            pltpu.VMEM((TILE, TILE), bf16),
            pltpu.VMEM((rows, 1), f32),
            pltpu.VMEM((rows, 1), f32),
            pltpu.VMEM((8, ch), f32),
            pltpu.VMEM((group1, 1, ch), f32),
            pltpu.VMEM((high, 1, ch), f32),
            dma((TAPS,)), dma, dma, dma,
            dma((7,)), dma((7,)), dma((7,)), dma((7,)),
            dma((group1,)), dma((group1,)), dma((high,)), dma((high,)), pltpu.SemaphoreType.REGULAR,
        ],
        compiler_params=pltpu.CompilerParams(
            collective_id=0, has_side_effects=True, vmem_limit_bytes=53_000_000),
        name="rc_block",
    )(*[pltpu.with_memory_space_constraint(x, pltpu.HBM) for x in (features, gain, conv_weight, cotangent)])
    return pl.pallas_call(
        hand_over,
        out_shape=(
            jax.ShapeDtypeStruct(conv.shape, bf16),
            jax.ShapeDtypeStruct(grad.shape, bf16),
            jax.ShapeDtypeStruct((ch,), f32),
        ),
        in_specs=[vmem_spec] * 3,
        out_specs=(hbm_spec, hbm_spec, vmem_spec),
        scratch_shapes=[dma((2,))],
        compiler_params=pltpu.CompilerParams(vmem_limit_bytes=4 * 1024 * 1024),
        name="hand_over",
    )(conv, grad, total)


def solution(mesh):
    return jax.shard_map(
        per_device,
        mesh=mesh,
        in_specs=(P("dp", "ctx", None), P(), P(), P("dp", "ctx", None)),
        out_specs=(P("dp", "ctx", None), P("dp", "ctx", None), P()),
        check_vma=False,
    )
```

```python
import functools
import math

import jax
import jax.numpy as jnp
from jax import lax
from jax.experimental import pallas as pl
from jax.experimental.pallas import tpu as pltpu
from jax.sharding import PartitionSpec as P

TAPS = 5
MID = TAPS // 2
SPAN = 8
EPS = 1e-06
TILE = 256
CHUNK = 16
LANES = 128
ROOT = math.sqrt(2.0 / math.pi)
CUBE = 0.044715
MESH = pl.DeviceIdType.MESH
ORDER = (1, 3, 0, 4, 2)
PARTNER, UP, DOWN = range(3)


def body(n_dp, n_ctx, rows_total, feat, gain_in, w, ct, conv_out, grad_out, gain_out,
         gain_ref, gain_v, acc, slope_gain, slope_normed, wv, xv, hh, fa, fb, csend, crecv, via, gg, flip_ref, inv_ref, spread_ref,
         part, sum1, sum2,
         w_sem, x_sem, g_sem, v_sem, ct_ssem, ct_rsem, c_ssem, c_rsem, s1_ssem, s1_rsem, s2_ssem, s2_rsem, know):
    rows, ch = xv.shape
    cout = ct.shape[-1]
    cut = rows * 5 // 8 // 16 * 16
    first, last, whole = pl.ds(0, cut), pl.ds(cut, rows - cut), pl.ds(0, rows)
    hops = n_ctx // SPAN
    me_dp = lax.axis_index("dp")
    me = lax.axis_index("ctx")
    high = SPAN // 2
    group1 = n_dp * hops * 2

    pos = me // hops
    odd = lax.rem(pos, 2)
    side = 2 * odd - 1
    pair = pos // 2
    near = me_dp * hops + lax.rem(me, hops)
    slot1 = odd * (n_dp * hops) + near

    def device(step):
        return {"dp": me_dp, "ctx": me + step * hops}

    def inside(step):
        return jnp.logical_and(pos + step >= 0, pos + step < SPAN)

    partner, up, down = device(-side), device(2 * side), device(-2 * side)
    has_up, has_down = inside(2 * side), inside(-2 * side)
    k_partner, k_diag, k_up, k_down = MID + side, MID - side, MID - 2 * side, MID + 2 * side

    copies_w = {}
    x_copy = pltpu.make_async_copy(feat.at[0], xv, x_sem)
    x_copy.start()
    v_copy = pltpu.make_async_copy(gain_in, gain_v, v_sem)
    v_copy.start()
    for k in ORDER:
        copies_w[k] = pltpu.make_async_copy(w.at[k], wv.at[k], w_sem.at[k])
        copies_w[k].start()
    g_copy = pltpu.make_async_copy(ct.at[0], gg.at[MID, whole], g_sem)
    g_copy.start()

    def peer1(j):
        other = lax.rem(slot1 + j, group1)
        rest = lax.rem(other, n_dp * hops)
        return {"dp": rest // hops, "ctx": (2 * pair + other // (n_dp * hops)) * hops + lax.rem(rest, hops)}

    def same_position(j):
        rest = lax.rem(near + j, n_dp * hops)
        return {"dp": rest // hops, "ctx": pos * hops + lax.rem(rest, hops)}

    def peer2(j):
        other = lax.rem(pair + j, high)
        return {"dp": me_dp, "ctx": (2 * other + odd) * hops + lax.rem(me, hops)}

    barrier = pltpu.get_barrier_semaphore()
    pl.semaphore_signal(barrier, inc=1, device_id=partner, device_id_type=MESH)
    @pl.when(has_up)
    def _():
        pl.semaphore_signal(barrier, inc=1, device_id=up, device_id_type=MESH)
    @pl.when(has_down)
    def _():
        pl.semaphore_signal(barrier, inc=1, device_id=down, device_id_type=MESH)
    for j in range(1, n_dp * hops):
        pl.semaphore_signal(barrier, inc=1, device_id=same_position(j), device_id_type=MESH)
    far = has_up.astype(jnp.int32) + has_down.astype(jnp.int32)
    count = n_dp * hops + far

    def move(src, dst, ssem, rsem, target):
        return pltpu.make_async_remote_copy(
            src_ref=src, dst_ref=dst, send_sem=ssem, recv_sem=rsem, device_id=target, device_id_type=MESH)

    def ct_move(n, src, slot, part_rows, target):
        return move(src.at[part_rows], gg.at[slot, part_rows], ct_ssem.at[n], ct_rsem.at[n], target)

    mine = ct.at[0]
    ct_partner = (ct_move(0, mine, k_diag, first, partner), ct_move(1, mine, k_diag, last, partner))
    ct_up = (ct_move(2, mine, k_down, first, up), ct_move(3, mine, k_down, last, up))
    ct_down = ct_move(4, mine, k_up, whole, down)
    ct_via_down = ct_move(5, gg.at[k_partner], k_diag, first, down)
    ct_via_partner = ct_move(6, gg.at[k_down], k_partner, last, partner)

    def c_move(n, k, dst, part_rows, target):
        return move(csend.at[k, part_rows], dst.at[part_rows], c_ssem.at[n], c_rsem.at[n], target)

    c_diag_up = c_move(0, k_diag, via, first, up)
    c_diag_partner = c_move(1, k_diag, via, last, partner)
    c_partner = (c_move(2, k_partner, crecv.at[PARTNER], first, partner),
                 c_move(3, k_partner, crecv.at[PARTNER], last, partner))
    c_down = (c_move(4, k_down, crecv.at[UP], first, down), c_move(5, k_down, crecv.at[UP], last, down))
    c_up = c_move(6, k_up, crecv.at[DOWN], whole, up)

    @pl.when(jnp.logical_not(has_up))
    def _():
        gg[k_up, whole, :] = jnp.zeros((rows, cout), jnp.bfloat16)
        gg[k_diag, whole, :] = jnp.zeros((rows, cout), jnp.bfloat16)
        crecv[UP] = jnp.zeros((rows, cout), jnp.bfloat16)
    @pl.when(jnp.logical_not(has_down))
    def _():
        gg[k_down, whole, :] = jnp.zeros((rows, cout), jnp.bfloat16)
        crecv[DOWN] = jnp.zeros((rows, cout), jnp.bfloat16)
        via[...] = jnp.zeros((rows, cout), jnp.bfloat16)

    r_iota = lax.broadcasted_iota(jnp.int32, (TILE, TILE), 0)
    c_iota = lax.broadcasted_iota(jnp.int32, (TILE, TILE), 1)
    flip_ref[...] = jnp.where(r_iota + c_iota == TILE - 1, 1.0, 0.0).astype(jnp.bfloat16)

    def flip_all(blocks):
        turned = jnp.dot(jnp.concatenate(blocks[::-1], axis=0), flip_ref[...], preferred_element_type=jnp.float32)
        return [turned[n * rows:(n + 1) * rows] for n in range(len(blocks))]

    n_out, n_in = cout // TILE, ch // TILE
    top, bottom = pl.ds(0, rows), pl.ds(rows, rows)
    tile = [pl.ds(j * TILE, TILE) for j in range(max(n_out, n_in))]

    v_copy.wait()
    gain_ref[...] = gain_v[...].reshape(1, ch)

    x_copy.wait()

    def activate(i):
        here = pl.ds(pl.multiple_of(i * CHUNK, CHUNK), CHUNK)
        wide = xv[here, :].astype(jnp.float32)
        inv = lax.rsqrt(jnp.mean(wide * wide, axis=-1, keepdims=True) + EPS)
        inv_ref[here, :] = inv
        gain = gain_ref[...]
        normed = wide * inv
        v = normed * gain
        square = v * v
        t = jnp.tanh(v * (ROOT + (ROOT * CUBE) * square))
        plus = 0.5 + 0.5 * t
        hh[here, :] = (v * plus).astype(jnp.bfloat16)
        slope = plus + v * (plus * (1.0 - t)) * (ROOT + (3.0 * ROOT * CUBE) * square)
        slope_gain[here, :] = slope * gain
        slope_normed[here, :] = slope * normed

    half = rows // CHUNK // 2
    pl.loop(0, half, unroll=2)(activate)

    pl.semaphore_wait(barrier, count)
    ct_partner[0].start()
    @pl.when(has_up)
    def _():
        ct_up[1].start()
    @pl.when(has_down)
    def _():
        ct_down.start()
    ct_partner[1].start()
    @pl.when(has_up)
    def _():
        ct_up[0].start()

    pl.loop(half, rows // CHUNK, unroll=2)(activate)

    for j, block in enumerate(flip_all([hh[top, tile[j]] for j in range(n_in)])):
        hh[bottom, tile[j]] = block.astype(jnp.bfloat16)

    def forward(k):
        for j in range(n_out):
            res = jnp.dot(hh[...], wv[k, :, tile[j]], preferred_element_type=jnp.float32)
            fa[k, :, tile[j]] = res[:rows]
            fb[k, :, tile[j]] = res[rows:].astype(jnp.bfloat16)

    def join(k):
        for j, block in enumerate(flip_all([fb[TAPS - 1 - k, :, tile[j]] for j in range(n_out)])):
            total = fa[k, :, tile[j]] + block
            fa[k, :, tile[j]] = total
            csend[k, :, tile[j]] = total.astype(jnp.bfloat16)

    def merge(k, part_rows):
        csend[k, part_rows, :] = (fa[k, part_rows, :] + via[part_rows, :].astype(jnp.float32)).astype(jnp.bfloat16)

    def flip_tap(k):
        for j, block in enumerate(flip_all([gg[k, top, tile[j]] for j in range(n_out)])):
            gg[TAPS - 1 - k, bottom, tile[j]] = block.astype(jnp.bfloat16)

    def backward(j, taps):
        return sum(lax.dot_general(
            gg[k], wv[k, tile[j], :], (((1,), (1,)), ((), ())), preferred_element_type=jnp.float32) for k in taps)

    for k in (1, 3):
        copies_w[k].wait()
    for k in (1, 3):
        forward(k)
    for k in (1, 3):
        join(k)
    @pl.when(has_up)
    def _():
        c_diag_up.start()
        c_diag_partner.start()
    c_partner[1].start()

    for k in (0, 4, 2):
        copies_w[k].wait()
    g_copy.wait()
    flip_tap(MID)
    ct_partner[0].wait_recv()
    @pl.when(has_down)
    def _():
        ct_via_down.start()
        ct_up[1].wait_recv()
        ct_via_partner.start()

    for j in range(n_in):
        acc[:, tile[j]] = backward(j, (MID,))

    forward(0)
    @pl.when(has_up)
    def _():
        ct_down.wait_recv()
    @pl.when(has_down)
    def _():
        ct_up[0].wait_recv()
    for k in (0, 4):
        flip_tap(k)
    for j in range(n_in):
        acc[:, tile[j]] = acc[:, tile[j]] + backward(j, (0, 4))
    @pl.when(has_up)
    def _():
        pl.semaphore_signal(know, inc=1, device_id=up, device_id_type=MESH)
    @pl.when(has_down)
    def _():
        pl.semaphore_signal(know, inc=1, device_id=down, device_id_type=MESH)

    forward(4)
    for k in (0, 4):
        join(k)
    @pl.when(has_up)
    def _():
        c_up.start()
    @pl.when(has_down)
    def _():
        c_down[0].start()

    ct_partner[1].wait_recv()
    @pl.when(has_up)
    def _():
        ct_via_down.wait_recv()
        ct_via_partner.wait_recv()
    for k in (1, 3):
        flip_tap(k)

    spread = jnp.zeros((rows, LANES), jnp.float32)
    for j in range(n_in // 2):
        pair_of = (j, n_in - 1 - j)
        totals = [acc[:, tile[i]] + backward(i, (1, 3)) for i in pair_of]
        turned = flip_all([total[rows:].astype(jnp.bfloat16) for total in totals])
        for i, total, block in zip(pair_of, totals, turned):
            grad = total[:rows] + block
            mixed = grad * slope_normed[:, tile[i]]
            part[:, tile[i]] = jnp.sum(mixed.reshape(rows // 8, 8, TILE), axis=0)
            acc[top, tile[i]] = grad * slope_gain[:, tile[i]]
            mixed = mixed * gain_ref[:, tile[i]]
            spread = spread + sum(mixed[:, n:n + LANES] for n in range(0, TILE, LANES))
    sum1[slot1] = jnp.sum(part[...], axis=0, keepdims=True)

    def s1_copy(j):
        return move(sum1.at[slot1], sum1.at[slot1], s1_ssem.at[j], s1_rsem.at[j], peer1(j))

    def s1_arrival(j):
        sender = lax.rem(slot1 + group1 - j, group1)
        return move(sum1.at[sender], sum1.at[sender], s1_ssem.at[j], s1_rsem.at[j], peer1(j))

    for j in range(1, group1):
        s1_copy(j).start()
    spread_ref[...] = jnp.sum(spread, axis=-1, keepdims=True) * (1.0 / ch)

    @pl.when(has_down)
    def _():
        c_diag_up.wait_recv()
    merge(k_partner, first)
    c_partner[0].start()
    @pl.when(has_down)
    def _():
        c_diag_partner.wait_recv()
        merge(k_down, last)
        c_down[1].start()
    forward(MID)

    @pl.loop(0, rows // CHUNK, unroll=2)
    def _(i):
        here = pl.ds(pl.multiple_of(i * CHUNK, CHUNK), CHUNK)
        inv = inv_ref[here, :]
        normed = xv[here, :].astype(jnp.float32) * inv
        grad_out[0, here, :] = (inv * (acc[here, :] - normed * spread_ref[here, :])).astype(jnp.bfloat16)

    for j in range(1, group1):
        s1_arrival(j).wait_recv()
    sum2[pair] = jnp.sum(sum1[...], axis=0)

    def s2_copy(j):
        return move(sum2.at[pair], sum2.at[pair], s2_ssem.at[j], s2_rsem.at[j], peer2(j))

    def s2_arrival(j):
        sender = lax.rem(pair + high - j, high)
        return move(sum2.at[sender], sum2.at[sender], s2_ssem.at[j], s2_rsem.at[j], peer2(j))

    pl.semaphore_wait(know, far)
    for j in range(1, high):
        s2_copy(j).start()

    c_partner[0].wait_recv()
    c_partner[1].wait_recv()
    @pl.when(has_up)
    def _():
        c_down[0].wait_recv()
        c_down[1].wait_recv()
    @pl.when(has_down)
    def _():
        c_up.wait_recv()

    for j, block in enumerate(flip_all([fb[MID, :, tile[j]] for j in range(n_out)])):
        total = fa[MID, :, tile[j]] + block
        for role in (PARTNER, UP, DOWN):
            total = total + crecv[role, :, tile[j]].astype(jnp.float32)
        conv_out[0, :, tile[j]] = total.astype(jnp.bfloat16)

    for j in range(1, high):
        s2_arrival(j).wait_recv()
    gain_out[...] = jnp.sum(sum2[...], axis=0) * (1.0 / math.sqrt(rows_total))

    for copy in (*ct_partner, *c_partner):
        copy.wait_send()
    @pl.when(has_up)
    def _():
        for copy in (*ct_up, c_diag_up, c_diag_partner, c_up):
            copy.wait_send()
    @pl.when(has_down)
    def _():
        for copy in (ct_down, ct_via_down, ct_via_partner, *c_down):
            copy.wait_send()
    for j in range(1, group1):
        s1_copy(j).wait_send()
    for j in range(1, high):
        s2_copy(j).wait_send()


def hand_over(conv, grad, total, conv_out, grad_out, total_out, sems):
    copies = [pltpu.make_async_copy(src, dst, sems.at[n])
              for n, (src, dst) in enumerate(((grad, grad_out), (conv, conv_out)))]
    for copy in copies:
        copy.start()
    total_out[...] = total[...].reshape(total_out.shape)
    for copy in copies:
        copy.wait()


def per_device(features, gain, conv_weight, cotangent):
    n_dp, n_ctx = lax.axis_size("dp"), lax.axis_size("ctx")
    lead, rows, ch = features.shape
    cout = cotangent.shape[-1]
    high = SPAN // 2
    group1 = n_dp * (n_ctx // SPAN) * 2
    rows_total = lead * rows * n_dp * n_ctx
    hbm_spec = pl.BlockSpec(memory_space=pltpu.HBM)
    vmem_spec = pl.BlockSpec(memory_space=pltpu.VMEM)
    bf16, f32 = jnp.bfloat16, jnp.float32
    dma = pltpu.SemaphoreType.DMA
    conv, grad, total = pl.pallas_call(
        functools.partial(body, n_dp, n_ctx, rows_total),
        out_shape=(
            jax.ShapeDtypeStruct((lead, rows, cout), bf16),
            jax.ShapeDtypeStruct((lead, rows, ch), bf16),
            jax.ShapeDtypeStruct((1, ch), f32),
        ),
        in_specs=[hbm_spec] * 4,
        out_specs=(vmem_spec, vmem_spec, vmem_spec),
        scratch_shapes=[
            pltpu.VMEM((1, ch), f32),
            pltpu.VMEM((ch,), f32),
            pltpu.VMEM((2 * rows, ch), f32),
            pltpu.VMEM((rows, ch), f32),
            pltpu.VMEM((rows, ch), f32),
            pltpu.VMEM((TAPS, ch, cout), bf16),
            pltpu.VMEM((rows, ch), bf16),
            pltpu.VMEM((2 * rows, ch), bf16),
            pltpu.VMEM((TAPS, rows, cout), f32),
            pltpu.VMEM((TAPS, rows, cout), bf16),
            pltpu.VMEM((TAPS, rows, cout), bf16),
            pltpu.VMEM((3, rows, cout), bf16),
            pltpu.VMEM((rows, cout), bf16),
            pltpu.VMEM((TAPS, 2 * rows, cout), bf16),
            pltpu.VMEM((TILE, TILE), bf16),
            pltpu.VMEM((rows, 1), f32),
            pltpu.VMEM((rows, 1), f32),
            pltpu.VMEM((8, ch), f32),
            pltpu.VMEM((group1, 1, ch), f32),
            pltpu.VMEM((high, 1, ch), f32),
            dma((TAPS,)), dma, dma, dma,
            dma((7,)), dma((7,)), dma((7,)), dma((7,)),
            dma((group1,)), dma((group1,)), dma((high,)), dma((high,)), pltpu.SemaphoreType.REGULAR,
        ],
        compiler_params=pltpu.CompilerParams(
            collective_id=0, has_side_effects=True, vmem_limit_bytes=53_000_000),
        name="rc_block",
    )(*[pltpu.with_memory_space_constraint(x, pltpu.HBM) for x in (features, gain, conv_weight, cotangent)])
    return pl.pallas_call(
        hand_over,
        out_shape=(
            jax.ShapeDtypeStruct(conv.shape, bf16),
            jax.ShapeDtypeStruct(grad.shape, bf16),
            jax.ShapeDtypeStruct((ch,), f32),
        ),
        in_specs=[vmem_spec] * 3,
        out_specs=(hbm_spec, hbm_spec, vmem_spec),
        scratch_shapes=[dma((2,))],
        compiler_params=pltpu.CompilerParams(vmem_limit_bytes=4 * 1024 * 1024),
        name="hand_over",
    )(conv, grad, total)


def solution(mesh):
    return jax.shard_map(
        per_device,
        mesh=mesh,
        in_specs=(P("dp", "ctx", None), P(), P(), P("dp", "ctx", None)),
        out_specs=(P("dp", "ctx", None), P("dp", "ctx", None), P()),
        check_vma=False,
    )
```

```python
import functools
import math

import jax
import jax.numpy as jnp
from jax import lax
from jax.experimental import pallas as pl
from jax.experimental.pallas import tpu as pltpu
from jax.sharding import PartitionSpec as P

TAPS = 5
MID = TAPS // 2
SPAN = 8
EPS = 1e-06
TILE = 256
CHUNK = 16
LANES = 128
ROOT = math.sqrt(2.0 / math.pi)
CUBE = 0.044715
MESH = pl.DeviceIdType.MESH
ORDER = (1, 3, 0, 4, 2)
PARTNER, UP, DOWN = range(3)


def body(n_dp, n_ctx, rows_total, feat, gain_in, w, ct, conv_out, grad_out, gain_out,
         gain_ref, gain_v, acc, slope_gain, slope_normed, wv, xv, hh, fa, fb, csend, crecv, via, gg, flip_ref, inv_ref, spread_ref,
         part, sum1, sum2,
         w_sem, x_sem, g_sem, v_sem, ct_ssem, ct_rsem, c_ssem, c_rsem, s1_ssem, s1_rsem, s2_ssem, s2_rsem, know):
    rows, ch = xv.shape
    cout = ct.shape[-1]
    cut = rows * 5 // 8 // 16 * 16
    first, last, whole = pl.ds(0, cut), pl.ds(cut, rows - cut), pl.ds(0, rows)
    hops = n_ctx // SPAN
    me_dp = lax.axis_index("dp")
    me = lax.axis_index("ctx")
    high = SPAN // 2
    group1 = n_dp * hops * 2

    pos = me // hops
    odd = lax.rem(pos, 2)
    side = 2 * odd - 1
    pair = pos // 2
    near = me_dp * hops + lax.rem(me, hops)
    slot1 = odd * (n_dp * hops) + near

    def device(step):
        return {"dp": me_dp, "ctx": me + step * hops}

    def inside(step):
        return jnp.logical_and(pos + step >= 0, pos + step < SPAN)

    partner, up, down = device(-side), device(2 * side), device(-2 * side)
    has_up, has_down = inside(2 * side), inside(-2 * side)
    k_partner, k_diag, k_up, k_down = MID + side, MID - side, MID - 2 * side, MID + 2 * side

    def peer1(j):
        other = lax.rem(slot1 + j, group1)
        rest = lax.rem(other, n_dp * hops)
        return {"dp": rest // hops, "ctx": (2 * pair + other // (n_dp * hops)) * hops + lax.rem(rest, hops)}

    def same_position(j):
        rest = lax.rem(near + j, n_dp * hops)
        return {"dp": rest // hops, "ctx": pos * hops + lax.rem(rest, hops)}

    def peer2(j):
        other = lax.rem(pair + j, high)
        return {"dp": me_dp, "ctx": (2 * other + odd) * hops + lax.rem(me, hops)}

    barrier = pltpu.get_barrier_semaphore()
    pl.semaphore_signal(barrier, inc=1, device_id=partner, device_id_type=MESH)
    @pl.when(has_up)
    def _():
        pl.semaphore_signal(barrier, inc=1, device_id=up, device_id_type=MESH)
    @pl.when(has_down)
    def _():
        pl.semaphore_signal(barrier, inc=1, device_id=down, device_id_type=MESH)
    for j in range(1, n_dp * hops):
        pl.semaphore_signal(barrier, inc=1, device_id=same_position(j), device_id_type=MESH)
    copies_w = {}
    x_copy = pltpu.make_async_copy(feat.at[0], xv, x_sem)
    x_copy.start()
    v_copy = pltpu.make_async_copy(gain_in, gain_v, v_sem)
    v_copy.start()
    for k in ORDER:
        copies_w[k] = pltpu.make_async_copy(w.at[k], wv.at[k], w_sem.at[k])
        copies_w[k].start()
    g_copy = pltpu.make_async_copy(ct.at[0], gg.at[MID, whole], g_sem)
    g_copy.start()

    far = has_up.astype(jnp.int32) + has_down.astype(jnp.int32)
    count = n_dp * hops + far

    def move(src, dst, ssem, rsem, target):
        return pltpu.make_async_remote_copy(
            src_ref=src, dst_ref=dst, send_sem=ssem, recv_sem=rsem, device_id=target, device_id_type=MESH)

    def ct_move(n, src, slot, part_rows, target):
        return move(src.at[part_rows], gg.at[slot, part_rows], ct_ssem.at[n], ct_rsem.at[n], target)

    mine = ct.at[0]
    ct_partner = (ct_move(0, mine, k_diag, first, partner), ct_move(1, mine, k_diag, last, partner))
    ct_up = (ct_move(2, mine, k_down, first, up), ct_move(3, mine, k_down, last, up))
    ct_down = ct_move(4, mine, k_up, whole, down)
    ct_via_down = ct_move(5, gg.at[k_partner], k_diag, first, down)
    ct_via_partner = ct_move(6, gg.at[k_down], k_partner, last, partner)

    def c_move(n, k, dst, part_rows, target):
        return move(csend.at[k, part_rows], dst.at[part_rows], c_ssem.at[n], c_rsem.at[n], target)

    c_diag_up = c_move(0, k_diag, via, first, up)
    c_diag_partner = c_move(1, k_diag, via, last, partner)
    c_partner = (c_move(2, k_partner, crecv.at[PARTNER], first, partner),
                 c_move(3, k_partner, crecv.at[PARTNER], last, partner))
    c_down = (c_move(4, k_down, crecv.at[UP], first, down), c_move(5, k_down, crecv.at[UP], last, down))
    c_up = c_move(6, k_up, crecv.at[DOWN], whole, up)

    pl.semaphore_wait(barrier, count)
    ct_partner[0].start()
    @pl.when(has_up)
    def _():
        ct_up[1].start()
    @pl.when(has_down)
    def _():
        ct_down.start()
    ct_partner[1].start()
    @pl.when(has_up)
    def _():
        ct_up[0].start()

    @pl.when(jnp.logical_not(has_up))
    def _():
        gg[k_up, whole, :] = jnp.zeros((rows, cout), jnp.bfloat16)
        gg[k_diag, whole, :] = jnp.zeros((rows, cout), jnp.bfloat16)
        crecv[UP] = jnp.zeros((rows, cout), jnp.bfloat16)
    @pl.when(jnp.logical_not(has_down))
    def _():
        gg[k_down, whole, :] = jnp.zeros((rows, cout), jnp.bfloat16)
        crecv[DOWN] = jnp.zeros((rows, cout), jnp.bfloat16)
        via[...] = jnp.zeros((rows, cout), jnp.bfloat16)

    r_iota = lax.broadcasted_iota(jnp.int32, (TILE, TILE), 0)
    c_iota = lax.broadcasted_iota(jnp.int32, (TILE, TILE), 1)
    flip_ref[...] = jnp.where(r_iota + c_iota == TILE - 1, 1.0, 0.0).astype(jnp.bfloat16)

    def flip_all(blocks):
        turned = jnp.dot(jnp.concatenate(blocks[::-1], axis=0), flip_ref[...], preferred_element_type=jnp.float32)
        return [turned[n * rows:(n + 1) * rows] for n in range(len(blocks))]

    n_out, n_in = cout // TILE, ch // TILE
    top, bottom = pl.ds(0, rows), pl.ds(rows, rows)
    tile = [pl.ds(j * TILE, TILE) for j in range(max(n_out, n_in))]

    v_copy.wait()
    gain_ref[...] = gain_v[...].reshape(1, ch)

    x_copy.wait()

    def activate(i):
        here = pl.ds(pl.multiple_of(i * CHUNK, CHUNK), CHUNK)
        wide = xv[here, :].astype(jnp.float32)
        inv = lax.rsqrt(jnp.mean(wide * wide, axis=-1, keepdims=True) + EPS)
        inv_ref[here, :] = inv
        gain = gain_ref[...]
        normed = wide * inv
        v = normed * gain
        square = v * v
        t = jnp.tanh(v * (ROOT + (ROOT * CUBE) * square))
        plus = 0.5 + 0.5 * t
        hh[here, :] = (v * plus).astype(jnp.bfloat16)
        slope = plus + v * (plus * (1.0 - t)) * (ROOT + (3.0 * ROOT * CUBE) * square)
        slope_gain[here, :] = slope * gain
        slope_normed[here, :] = slope * normed

    pl.loop(0, rows // CHUNK, unroll=2)(activate)

    for j, block in enumerate(flip_all([hh[top, tile[j]] for j in range(n_in)])):
        hh[bottom, tile[j]] = block.astype(jnp.bfloat16)

    def forward(k):
        for j in range(n_out):
            res = jnp.dot(hh[...], wv[k, :, tile[j]], preferred_element_type=jnp.float32)
            fa[k, :, tile[j]] = res[:rows]
            fb[k, :, tile[j]] = res[rows:].astype(jnp.bfloat16)

    def join(k):
        for j, block in enumerate(flip_all([fb[TAPS - 1 - k, :, tile[j]] for j in range(n_out)])):
            total = fa[k, :, tile[j]] + block
            fa[k, :, tile[j]] = total
            csend[k, :, tile[j]] = total.astype(jnp.bfloat16)

    def merge(k, part_rows):
        csend[k, part_rows, :] = (fa[k, part_rows, :] + via[part_rows, :].astype(jnp.float32)).astype(jnp.bfloat16)

    def flip_tap(k):
        for j, block in enumerate(flip_all([gg[k, top, tile[j]] for j in range(n_out)])):
            gg[TAPS - 1 - k, bottom, tile[j]] = block.astype(jnp.bfloat16)

    def backward(j, taps):
        return sum(lax.dot_general(
            gg[k], wv[k, tile[j], :], (((1,), (1,)), ((), ())), preferred_element_type=jnp.float32) for k in taps)

    for k in (1, 3):
        copies_w[k].wait()
    for k in (1, 3):
        forward(k)
    for k in (1, 3):
        join(k)
    @pl.when(has_up)
    def _():
        c_diag_up.start()
        c_diag_partner.start()
    c_partner[1].start()

    for k in (0, 4, 2):
        copies_w[k].wait()
    g_copy.wait()
    flip_tap(MID)
    ct_partner[0].wait_recv()
    @pl.when(has_down)
    def _():
        ct_via_down.start()
        ct_up[1].wait_recv()
        ct_via_partner.start()

    for j in range(n_in):
        acc[:, tile[j]] = backward(j, (MID,))

    forward(0)
    @pl.when(has_up)
    def _():
        ct_down.wait_recv()
    @pl.when(has_down)
    def _():
        ct_up[0].wait_recv()
    for k in (0, 4):
        flip_tap(k)
    for j in range(n_in):
        acc[:, tile[j]] = acc[:, tile[j]] + backward(j, (0, 4))
    @pl.when(has_up)
    def _():
        pl.semaphore_signal(know, inc=1, device_id=up, device_id_type=MESH)
    @pl.when(has_down)
    def _():
        pl.semaphore_signal(know, inc=1, device_id=down, device_id_type=MESH)

    forward(4)
    for k in (0, 4):
        join(k)
    @pl.when(has_up)
    def _():
        c_up.start()
    @pl.when(has_down)
    def _():
        c_down[0].start()

    ct_partner[1].wait_recv()
    @pl.when(has_up)
    def _():
        ct_via_down.wait_recv()
        ct_via_partner.wait_recv()
    for k in (1, 3):
        flip_tap(k)

    spread = jnp.zeros((rows, LANES), jnp.float32)
    for j in range(n_in // 2):
        pair_of = (j, n_in - 1 - j)
        totals = [acc[:, tile[i]] + backward(i, (1, 3)) for i in pair_of]
        turned = flip_all([total[rows:].astype(jnp.bfloat16) for total in totals])
        for i, total, block in zip(pair_of, totals, turned):
            grad = total[:rows] + block
            mixed = grad * slope_normed[:, tile[i]]
            part[:, tile[i]] = jnp.sum(mixed.reshape(rows // 8, 8, TILE), axis=0)
            acc[top, tile[i]] = grad * slope_gain[:, tile[i]]
            mixed = mixed * gain_ref[:, tile[i]]
            spread = spread + sum(mixed[:, n:n + LANES] for n in range(0, TILE, LANES))
    sum1[slot1] = jnp.sum(part[...], axis=0, keepdims=True)

    def s1_copy(j):
        return move(sum1.at[slot1], sum1.at[slot1], s1_ssem.at[j], s1_rsem.at[j], peer1(j))

    def s1_arrival(j):
        sender = lax.rem(slot1 + group1 - j, group1)
        return move(sum1.at[sender], sum1.at[sender], s1_ssem.at[j], s1_rsem.at[j], peer1(j))

    for j in range(1, group1):
        s1_copy(j).start()
    spread_ref[...] = jnp.sum(spread, axis=-1, keepdims=True) * (1.0 / ch)

    @pl.when(has_down)
    def _():
        c_diag_up.wait_recv()
    merge(k_partner, first)
    c_partner[0].start()
    @pl.when(has_down)
    def _():
        c_diag_partner.wait_recv()
        merge(k_down, last)
        c_down[1].start()
    forward(MID)

    @pl.loop(0, rows // CHUNK, unroll=2)
    def _(i):
        here = pl.ds(pl.multiple_of(i * CHUNK, CHUNK), CHUNK)
        inv = inv_ref[here, :]
        normed = xv[here, :].astype(jnp.float32) * inv
        grad_out[0, here, :] = (inv * (acc[here, :] - normed * spread_ref[here, :])).astype(jnp.bfloat16)

    for j in range(1, group1):
        s1_arrival(j).wait_recv()
    sum2[pair] = jnp.sum(sum1[...], axis=0)

    def s2_copy(j):
        return move(sum2.at[pair], sum2.at[pair], s2_ssem.at[j], s2_rsem.at[j], peer2(j))

    def s2_arrival(j):
        sender = lax.rem(pair + high - j, high)
        return move(sum2.at[sender], sum2.at[sender], s2_ssem.at[j], s2_rsem.at[j], peer2(j))

    pl.semaphore_wait(know, far)
    for j in range(1, high):
        s2_copy(j).start()

    c_partner[0].wait_recv()
    c_partner[1].wait_recv()
    @pl.when(has_up)
    def _():
        c_down[0].wait_recv()
        c_down[1].wait_recv()
    @pl.when(has_down)
    def _():
        c_up.wait_recv()

    for j, block in enumerate(flip_all([fb[MID, :, tile[j]] for j in range(n_out)])):
        total = fa[MID, :, tile[j]] + block
        for role in (PARTNER, UP, DOWN):
            total = total + crecv[role, :, tile[j]].astype(jnp.float32)
        conv_out[0, :, tile[j]] = total.astype(jnp.bfloat16)

    for j in range(1, high):
        s2_arrival(j).wait_recv()
    gain_out[...] = jnp.sum(sum2[...], axis=0) * (1.0 / math.sqrt(rows_total))

    for copy in (*ct_partner, *c_partner):
        copy.wait_send()
    @pl.when(has_up)
    def _():
        for copy in (*ct_up, c_diag_up, c_diag_partner, c_up):
            copy.wait_send()
    @pl.when(has_down)
    def _():
        for copy in (ct_down, ct_via_down, ct_via_partner, *c_down):
            copy.wait_send()
    for j in range(1, group1):
        s1_copy(j).wait_send()
    for j in range(1, high):
        s2_copy(j).wait_send()


def hand_over(conv, grad, total, conv_out, grad_out, total_out, sems):
    copies = [pltpu.make_async_copy(src, dst, sems.at[n])
              for n, (src, dst) in enumerate(((grad, grad_out), (conv, conv_out)))]
    for copy in copies:
        copy.start()
    total_out[...] = total[...].reshape(total_out.shape)
    for copy in copies:
        copy.wait()


def per_device(features, gain, conv_weight, cotangent):
    n_dp, n_ctx = lax.axis_size("dp"), lax.axis_size("ctx")
    lead, rows, ch = features.shape
    cout = cotangent.shape[-1]
    high = SPAN // 2
    group1 = n_dp * (n_ctx // SPAN) * 2
    rows_total = lead * rows * n_dp * n_ctx
    hbm_spec = pl.BlockSpec(memory_space=pltpu.HBM)
    vmem_spec = pl.BlockSpec(memory_space=pltpu.VMEM)
    bf16, f32 = jnp.bfloat16, jnp.float32
    dma = pltpu.SemaphoreType.DMA
    conv, grad, total = pl.pallas_call(
        functools.partial(body, n_dp, n_ctx, rows_total),
        out_shape=(
            jax.ShapeDtypeStruct((lead, rows, cout), bf16),
            jax.ShapeDtypeStruct((lead, rows, ch), bf16),
            jax.ShapeDtypeStruct((1, ch), f32),
        ),
        in_specs=[hbm_spec] * 4,
        out_specs=(vmem_spec, vmem_spec, vmem_spec),
        scratch_shapes=[
            pltpu.VMEM((1, ch), f32),
            pltpu.VMEM((ch,), f32),
            pltpu.VMEM((2 * rows, ch), f32),
            pltpu.VMEM((rows, ch), f32),
            pltpu.VMEM((rows, ch), f32),
            pltpu.VMEM((TAPS, ch, cout), bf16),
            pltpu.VMEM((rows, ch), bf16),
            pltpu.VMEM((2 * rows, ch), bf16),
            pltpu.VMEM((TAPS, rows, cout), f32),
            pltpu.VMEM((TAPS, rows, cout), bf16),
            pltpu.VMEM((TAPS, rows, cout), bf16),
            pltpu.VMEM((3, rows, cout), bf16),
            pltpu.VMEM((rows, cout), bf16),
            pltpu.VMEM((TAPS, 2 * rows, cout), bf16),
            pltpu.VMEM((TILE, TILE), bf16),
            pltpu.VMEM((rows, 1), f32),
            pltpu.VMEM((rows, 1), f32),
            pltpu.VMEM((8, ch), f32),
            pltpu.VMEM((group1, 1, ch), f32),
            pltpu.VMEM((high, 1, ch), f32),
            dma((TAPS,)), dma, dma, dma,
            dma((7,)), dma((7,)), dma((7,)), dma((7,)),
            dma((group1,)), dma((group1,)), dma((high,)), dma((high,)), pltpu.SemaphoreType.REGULAR,
        ],
        compiler_params=pltpu.CompilerParams(
            collective_id=0, has_side_effects=True, vmem_limit_bytes=53_000_000),
        name="rc_block",
    )(*[pltpu.with_memory_space_constraint(x, pltpu.HBM) for x in (features, gain, conv_weight, cotangent)])
    return pl.pallas_call(
        hand_over,
        out_shape=(
            jax.ShapeDtypeStruct(conv.shape, bf16),
            jax.ShapeDtypeStruct(grad.shape, bf16),
            jax.ShapeDtypeStruct((ch,), f32),
        ),
        in_specs=[vmem_spec] * 3,
        out_specs=(hbm_spec, hbm_spec, vmem_spec),
        scratch_shapes=[dma((2,))],
        compiler_params=pltpu.CompilerParams(vmem_limit_bytes=4 * 1024 * 1024),
        name="hand_over",
    )(conv, grad, total)


def solution(mesh):
    return jax.shard_map(
        per_device,
        mesh=mesh,
        in_specs=(P("dp", "ctx", None), P(), P(), P("dp", "ctx", None)),
        out_specs=(P("dp", "ctx", None), P("dp", "ctx", None), P()),
        check_vma=False,
    )
```

```python
import functools
import math

import jax
import jax.numpy as jnp
from jax import lax
from jax.experimental import pallas as pl
from jax.experimental.pallas import tpu as pltpu
from jax.sharding import PartitionSpec as P

TAPS = 5
MID = TAPS // 2
SPAN = 8
EPS = 1e-06
TILE = 256
CHUNK = 16
LANES = 128
ROOT = math.sqrt(2.0 / math.pi)
CUBE = 0.044715
MESH = pl.DeviceIdType.MESH
ORDER = (1, 3, 0, 4, 2)
PARTNER, UP, DOWN = range(3)


def body(n_dp, n_ctx, rows_total, feat, gain_in, w, ct, conv_out, grad_out, gain_out,
         gain_ref, gain_v, acc, slope_gain, slope_normed, wv, xv, hh, fa, fb, csend, crecv, via, gg, flip_ref, inv_ref, spread_ref,
         part, sum1, sum2,
         w_sem, x_sem, g_sem, v_sem, ct_ssem, ct_rsem, c_ssem, c_rsem, s1_ssem, s1_rsem, s2_ssem, s2_rsem, know):
    rows, ch = xv.shape
    cout = ct.shape[-1]
    cut = rows * 5 // 8 // 16 * 16
    first, last, whole = pl.ds(0, cut), pl.ds(cut, rows - cut), pl.ds(0, rows)
    hops = n_ctx // SPAN
    me_dp = lax.axis_index("dp")
    me = lax.axis_index("ctx")
    high = SPAN // 2
    group1 = n_dp * hops * 2

    pos = me // hops
    odd = lax.rem(pos, 2)
    side = 2 * odd - 1
    pair = pos // 2
    near = me_dp * hops + lax.rem(me, hops)
    slot1 = odd * (n_dp * hops) + near

    def device(step):
        return {"dp": me_dp, "ctx": me + step * hops}

    def inside(step):
        return jnp.logical_and(pos + step >= 0, pos + step < SPAN)

    partner, up, down = device(-side), device(2 * side), device(-2 * side)
    has_up, has_down = inside(2 * side), inside(-2 * side)
    k_partner, k_diag, k_up, k_down = MID + side, MID - side, MID - 2 * side, MID + 2 * side

    def peer1(j):
        other = lax.rem(slot1 + j, group1)
        rest = lax.rem(other, n_dp * hops)
        return {"dp": rest // hops, "ctx": (2 * pair + other // (n_dp * hops)) * hops + lax.rem(rest, hops)}

    def same_position(j):
        rest = lax.rem(near + j, n_dp * hops)
        return {"dp": rest // hops, "ctx": pos * hops + lax.rem(rest, hops)}

    def peer2(j):
        other = lax.rem(pair + j, high)
        return {"dp": me_dp, "ctx": (2 * other + odd) * hops + lax.rem(me, hops)}

    barrier = pltpu.get_barrier_semaphore()
    pl.semaphore_signal(barrier, inc=1, device_id=partner, device_id_type=MESH)
    @pl.when(has_up)
    def _():
        pl.semaphore_signal(barrier, inc=1, device_id=up, device_id_type=MESH)
    @pl.when(has_down)
    def _():
        pl.semaphore_signal(barrier, inc=1, device_id=down, device_id_type=MESH)
    for j in range(1, n_dp * hops):
        pl.semaphore_signal(barrier, inc=1, device_id=same_position(j), device_id_type=MESH)
    copies_w = {}
    x_copy = pltpu.make_async_copy(feat.at[0], xv, x_sem)
    x_copy.start()
    v_copy = pltpu.make_async_copy(gain_in, gain_v, v_sem)
    v_copy.start()
    for k in ORDER:
        copies_w[k] = pltpu.make_async_copy(w.at[k], wv.at[k], w_sem.at[k])
        copies_w[k].start()
    g_copy = pltpu.make_async_copy(ct.at[0], gg.at[MID, whole], g_sem)
    g_copy.start()

    far = has_up.astype(jnp.int32) + has_down.astype(jnp.int32)
    count = n_dp * hops + far

    def move(src, dst, ssem, rsem, target):
        return pltpu.make_async_remote_copy(
            src_ref=src, dst_ref=dst, send_sem=ssem, recv_sem=rsem, device_id=target, device_id_type=MESH)

    def ct_move(n, src, slot, part_rows, target):
        return move(src.at[part_rows], gg.at[slot, part_rows], ct_ssem.at[n], ct_rsem.at[n], target)

    mine = ct.at[0]
    ct_partner = (ct_move(0, mine, k_diag, first, partner), ct_move(1, mine, k_diag, last, partner))
    ct_up = (ct_move(2, mine, k_down, first, up), ct_move(3, mine, k_down, last, up))
    ct_down = ct_move(4, mine, k_up, whole, down)
    ct_via_down = ct_move(5, gg.at[k_partner], k_diag, first, down)
    ct_via_partner = ct_move(6, gg.at[k_down], k_partner, last, partner)

    def c_move(n, k, dst, part_rows, target):
        return move(csend.at[k, part_rows], dst.at[part_rows], c_ssem.at[n], c_rsem.at[n], target)

    c_diag_up = c_move(0, k_diag, via, first, up)
    c_diag_partner = c_move(1, k_diag, via, last, partner)
    c_partner = (c_move(2, k_partner, crecv.at[PARTNER], first, partner),
                 c_move(3, k_partner, crecv.at[PARTNER], last, partner))
    c_down = (c_move(4, k_down, crecv.at[UP], first, down), c_move(5, k_down, crecv.at[UP], last, down))
    c_up = c_move(6, k_up, crecv.at[DOWN], whole, up)

    pl.semaphore_wait(barrier, count)
    ct_partner[0].start()
    @pl.when(has_up)
    def _():
        ct_up[1].start()
    @pl.when(has_down)
    def _():
        ct_down.start()
    ct_partner[1].start()
    @pl.when(has_up)
    def _():
        ct_up[0].start()

    @pl.when(jnp.logical_not(has_up))
    def _():
        gg[k_up, whole, :] = jnp.zeros((rows, cout), jnp.bfloat16)
        gg[k_diag, whole, :] = jnp.zeros((rows, cout), jnp.bfloat16)
        crecv[UP] = jnp.zeros((rows, cout), jnp.bfloat16)
    @pl.when(jnp.logical_not(has_down))
    def _():
        gg[k_down, whole, :] = jnp.zeros((rows, cout), jnp.bfloat16)
        crecv[DOWN] = jnp.zeros((rows, cout), jnp.bfloat16)
        via[...] = jnp.zeros((rows, cout), jnp.bfloat16)

    r_iota = lax.broadcasted_iota(jnp.int32, (TILE, TILE), 0)
    c_iota = lax.broadcasted_iota(jnp.int32, (TILE, TILE), 1)
    flip_ref[...] = jnp.where(r_iota + c_iota == TILE - 1, 1.0, 0.0).astype(jnp.bfloat16)

    def flip_all(blocks):
        turned = jnp.dot(jnp.concatenate(blocks[::-1], axis=0), flip_ref[...], preferred_element_type=jnp.float32)
        return [turned[n * rows:(n + 1) * rows] for n in range(len(blocks))]

    n_out, n_in = cout // TILE, ch // TILE
    top, bottom = pl.ds(0, rows), pl.ds(rows, rows)
    tile = [pl.ds(j * TILE, TILE) for j in range(max(n_out, n_in))]

    v_copy.wait()
    gain_ref[...] = gain_v[...].reshape(1, ch)

    x_copy.wait()

    def activate(i):
        here = pl.ds(pl.multiple_of(i * CHUNK, CHUNK), CHUNK)
        wide = xv[here, :].astype(jnp.float32)
        inv = lax.rsqrt(jnp.mean(wide * wide, axis=-1, keepdims=True) + EPS)
        inv_ref[here, :] = inv
        gain = gain_ref[...]
        normed = wide * inv
        v = normed * gain
        square = v * v
        t = jnp.tanh(v * (ROOT + (ROOT * CUBE) * square))
        plus = 0.5 + 0.5 * t
        hh[here, :] = (v * plus).astype(jnp.bfloat16)
        slope = plus + v * (plus * (1.0 - t)) * (ROOT + (3.0 * ROOT * CUBE) * square)
        slope_gain[here, :] = slope * gain
        slope_normed[here, :] = slope * normed

    pl.loop(0, rows // CHUNK, unroll=2)(activate)

    for j, block in enumerate(flip_all([hh[top, tile[j]] for j in range(n_in)])):
        hh[bottom, tile[j]] = block.astype(jnp.bfloat16)

    def forward(k):
        for j in range(n_out):
            res = jnp.dot(hh[...], wv[k, :, tile[j]], preferred_element_type=jnp.float32)
            fa[k, :, tile[j]] = res[:rows]
            fb[k, :, tile[j]] = res[rows:].astype(jnp.bfloat16)

    def join(k):
        for j, block in enumerate(flip_all([fb[TAPS - 1 - k, :, tile[j]] for j in range(n_out)])):
            total = fa[k, :, tile[j]] + block
            fa[k, :, tile[j]] = total
            csend[k, :, tile[j]] = total.astype(jnp.bfloat16)

    def merge(k, part_rows):
        csend[k, part_rows, :] = (fa[k, part_rows, :] + via[part_rows, :].astype(jnp.float32)).astype(jnp.bfloat16)

    def flip_tap(k):
        for j, block in enumerate(flip_all([gg[k, top, tile[j]] for j in range(n_out)])):
            gg[TAPS - 1 - k, bottom, tile[j]] = block.astype(jnp.bfloat16)

    def backward(j, taps):
        return sum(lax.dot_general(
            gg[k], wv[k, tile[j], :], (((1,), (1,)), ((), ())), preferred_element_type=jnp.float32) for k in taps)

    for k in (1, 3):
        copies_w[k].wait()
    for k in (1, 3):
        forward(k)
    for k in (1, 3):
        join(k)
    for k in (0, 4, 2):
        copies_w[k].wait()
    g_copy.wait()
    flip_tap(MID)
    ct_partner[0].wait_recv()
    @pl.when(has_down)
    def _():
        ct_via_down.start()
        ct_up[1].wait_recv()
        ct_via_partner.start()

    @pl.when(has_up)
    def _():
        c_diag_up.start()
        c_diag_partner.start()
    c_partner[1].start()

    for j in range(n_in):
        acc[:, tile[j]] = backward(j, (MID,))

    forward(0)
    @pl.when(has_up)
    def _():
        ct_down.wait_recv()
    @pl.when(has_down)
    def _():
        ct_up[0].wait_recv()
    for k in (0, 4):
        flip_tap(k)
    for j in range(n_in):
        acc[:, tile[j]] = acc[:, tile[j]] + backward(j, (0, 4))
    @pl.when(has_up)
    def _():
        pl.semaphore_signal(know, inc=1, device_id=up, device_id_type=MESH)
    @pl.when(has_down)
    def _():
        pl.semaphore_signal(know, inc=1, device_id=down, device_id_type=MESH)

    forward(4)
    for k in (0, 4):
        join(k)
    @pl.when(has_up)
    def _():
        c_up.start()
    @pl.when(has_down)
    def _():
        c_down[0].start()

    ct_partner[1].wait_recv()
    @pl.when(has_up)
    def _():
        ct_via_down.wait_recv()
        ct_via_partner.wait_recv()
    for k in (1, 3):
        flip_tap(k)

    spread = jnp.zeros((rows, LANES), jnp.float32)
    for j in range(n_in // 2):
        pair_of = (j, n_in - 1 - j)
        totals = [acc[:, tile[i]] + backward(i, (1, 3)) for i in pair_of]
        turned = flip_all([total[rows:].astype(jnp.bfloat16) for total in totals])
        for i, total, block in zip(pair_of, totals, turned):
            grad = total[:rows] + block
            mixed = grad * slope_normed[:, tile[i]]
            part[:, tile[i]] = jnp.sum(mixed.reshape(rows // 8, 8, TILE), axis=0)
            acc[top, tile[i]] = grad * slope_gain[:, tile[i]]
            mixed = mixed * gain_ref[:, tile[i]]
            spread = spread + sum(mixed[:, n:n + LANES] for n in range(0, TILE, LANES))
    sum1[slot1] = jnp.sum(part[...], axis=0, keepdims=True)

    def s1_copy(j):
        return move(sum1.at[slot1], sum1.at[slot1], s1_ssem.at[j], s1_rsem.at[j], peer1(j))

    def s1_arrival(j):
        sender = lax.rem(slot1 + group1 - j, group1)
        return move(sum1.at[sender], sum1.at[sender], s1_ssem.at[j], s1_rsem.at[j], peer1(j))

    for j in range(1, group1):
        s1_copy(j).start()
    spread_ref[...] = jnp.sum(spread, axis=-1, keepdims=True) * (1.0 / ch)

    @pl.when(has_down)
    def _():
        c_diag_up.wait_recv()
    merge(k_partner, first)
    c_partner[0].start()
    @pl.when(has_down)
    def _():
        c_diag_partner.wait_recv()
        merge(k_down, last)
        c_down[1].start()
    forward(MID)

    @pl.loop(0, rows // CHUNK, unroll=2)
    def _(i):
        here = pl.ds(pl.multiple_of(i * CHUNK, CHUNK), CHUNK)
        inv = inv_ref[here, :]
        normed = xv[here, :].astype(jnp.float32) * inv
        grad_out[0, here, :] = (inv * (acc[here, :] - normed * spread_ref[here, :])).astype(jnp.bfloat16)

    for j in range(1, group1):
        s1_arrival(j).wait_recv()
    sum2[pair] = jnp.sum(sum1[...], axis=0)

    def s2_copy(j):
        return move(sum2.at[pair], sum2.at[pair], s2_ssem.at[j], s2_rsem.at[j], peer2(j))

    def s2_arrival(j):
        sender = lax.rem(pair + high - j, high)
        return move(sum2.at[sender], sum2.at[sender], s2_ssem.at[j], s2_rsem.at[j], peer2(j))

    pl.semaphore_wait(know, far)
    for j in range(1, high):
        s2_copy(j).start()

    c_partner[0].wait_recv()
    c_partner[1].wait_recv()
    @pl.when(has_up)
    def _():
        c_down[0].wait_recv()
        c_down[1].wait_recv()
    @pl.when(has_down)
    def _():
        c_up.wait_recv()

    for j, block in enumerate(flip_all([fb[MID, :, tile[j]] for j in range(n_out)])):
        total = fa[MID, :, tile[j]] + block
        for role in (PARTNER, UP, DOWN):
            total = total + crecv[role, :, tile[j]].astype(jnp.float32)
        conv_out[0, :, tile[j]] = total.astype(jnp.bfloat16)

    for j in range(1, high):
        s2_arrival(j).wait_recv()
    gain_out[...] = jnp.sum(sum2[...], axis=0) * (1.0 / math.sqrt(rows_total))

    for copy in (*ct_partner, *c_partner):
        copy.wait_send()
    @pl.when(has_up)
    def _():
        for copy in (*ct_up, c_diag_up, c_diag_partner, c_up):
            copy.wait_send()
    @pl.when(has_down)
    def _():
        for copy in (ct_down, ct_via_down, ct_via_partner, *c_down):
            copy.wait_send()
    for j in range(1, group1):
        s1_copy(j).wait_send()
    for j in range(1, high):
        s2_copy(j).wait_send()


def hand_over(conv, grad, total, conv_out, grad_out, total_out, sems):
    copies = [pltpu.make_async_copy(src, dst, sems.at[n])
              for n, (src, dst) in enumerate(((grad, grad_out), (conv, conv_out)))]
    for copy in copies:
        copy.start()
    total_out[...] = total[...].reshape(total_out.shape)
    for copy in copies:
        copy.wait()


def per_device(features, gain, conv_weight, cotangent):
    n_dp, n_ctx = lax.axis_size("dp"), lax.axis_size("ctx")
    lead, rows, ch = features.shape
    cout = cotangent.shape[-1]
    high = SPAN // 2
    group1 = n_dp * (n_ctx // SPAN) * 2
    rows_total = lead * rows * n_dp * n_ctx
    hbm_spec = pl.BlockSpec(memory_space=pltpu.HBM)
    vmem_spec = pl.BlockSpec(memory_space=pltpu.VMEM)
    bf16, f32 = jnp.bfloat16, jnp.float32
    dma = pltpu.SemaphoreType.DMA
    conv, grad, total = pl.pallas_call(
        functools.partial(body, n_dp, n_ctx, rows_total),
        out_shape=(
            jax.ShapeDtypeStruct((lead, rows, cout), bf16),
            jax.ShapeDtypeStruct((lead, rows, ch), bf16),
            jax.ShapeDtypeStruct((1, ch), f32),
        ),
        in_specs=[hbm_spec] * 4,
        out_specs=(vmem_spec, vmem_spec, vmem_spec),
        scratch_shapes=[
            pltpu.VMEM((1, ch), f32),
            pltpu.VMEM((ch,), f32),
            pltpu.VMEM((2 * rows, ch), f32),
            pltpu.VMEM((rows, ch), f32),
            pltpu.VMEM((rows, ch), f32),
            pltpu.VMEM((TAPS, ch, cout), bf16),
            pltpu.VMEM((rows, ch), bf16),
            pltpu.VMEM((2 * rows, ch), bf16),
            pltpu.VMEM((TAPS, rows, cout), f32),
            pltpu.VMEM((TAPS, rows, cout), bf16),
            pltpu.VMEM((TAPS, rows, cout), bf16),
            pltpu.VMEM((3, rows, cout), bf16),
            pltpu.VMEM((rows, cout), bf16),
            pltpu.VMEM((TAPS, 2 * rows, cout), bf16),
            pltpu.VMEM((TILE, TILE), bf16),
            pltpu.VMEM((rows, 1), f32),
            pltpu.VMEM((rows, 1), f32),
            pltpu.VMEM((8, ch), f32),
            pltpu.VMEM((group1, 1, ch), f32),
            pltpu.VMEM((high, 1, ch), f32),
            dma((TAPS,)), dma, dma, dma,
            dma((7,)), dma((7,)), dma((7,)), dma((7,)),
            dma((group1,)), dma((group1,)), dma((high,)), dma((high,)), pltpu.SemaphoreType.REGULAR,
        ],
        compiler_params=pltpu.CompilerParams(
            collective_id=0, has_side_effects=True, vmem_limit_bytes=53_000_000),
        name="rc_block",
    )(*[pltpu.with_memory_space_constraint(x, pltpu.HBM) for x in (features, gain, conv_weight, cotangent)])
    return pl.pallas_call(
        hand_over,
        out_shape=(
            jax.ShapeDtypeStruct(conv.shape, bf16),
            jax.ShapeDtypeStruct(grad.shape, bf16),
            jax.ShapeDtypeStruct((ch,), f32),
        ),
        in_specs=[vmem_spec] * 3,
        out_specs=(hbm_spec, hbm_spec, vmem_spec),
        scratch_shapes=[dma((2,))],
        compiler_params=pltpu.CompilerParams(vmem_limit_bytes=4 * 1024 * 1024),
        name="hand_over",
    )(conv, grad, total)


def solution(mesh):
    return jax.shard_map(
        per_device,
        mesh=mesh,
        in_specs=(P("dp", "ctx", None), P(), P(), P("dp", "ctx", None)),
        out_specs=(P("dp", "ctx", None), P("dp", "ctx", None), P()),
        check_vma=False,
    )
```
